32 devices in a mesh: dp: 8 (over z, x), mp: 4 (over y, core).
Axes of the slice: x: 2, y: 2, z: 4, core: 2. Of those that a mesh axis runs over, the one named last changes fastest.
Arguments:
- conv_in: bfloat16 [16384, 1024], P('dp'), may hold values from -6 to 6
- conv_weight: bfloat16 [1024, 512], P(None, 'mp'), may hold values from -0.1875 to 0.1875
- feature_gain: float32 [512], replicated, may hold values from 0.1 to 1.9
- proj_weight: bfloat16 [512, 1024], replicated, may hold values from -0.25 to 0.25
- block_gain: float32 [1024], replicated, may hold values from 0.1 to 1.9
- w_in: bfloat16 [1024, 4096], P(None, 'mp'), may hold values from -0.1875 to 0.1875
- w_out: bfloat16 [1024, 4096], P(None, 'mp'), may hold values from -0.09375 to 0.09375
- cotangent: bfloat16 [16384, 1024], P('dp'), may hold values from -0.0625 to 0.0625
- send_index: int32 [16384], P('dp'), may hold values from 0 to 2047, as said below
- slot_valid: int32 [16384], P('dp'), may hold values from 0 to 1, as said below
Outputs:
- grad_conv_weight: float32 [1024, 512], P('dp', 'mp')
- grad_proj_weight: float32 [512, 1024], P('dp', 'mp')
- grad_w_in: float32 [1024, 4096], P('dp', 'mp')
- grad_w_out: float32 [1024, 4096], P('dp', 'mp')
The draws below stay inside these ranges and needn't reach their ends.
Inputs may be any that keep to these rules, and one draw needn't show every extreme that they name: `send_index`: the 2048 entries held by one index of dp are a permutation of 0 to 2047; entry e * 256 + j names the local frame sent to slot j of index e. `slot_valid`: slot j of the block from source s on index e is 1 exactly when the frame it receives lies inside the source's clips; a source's frames inside clips are its first ones, at least 512 of them, and some source has all 2048.
All inputs are finite; a program needn't handle non-finite values.
Results may differ from the reference program's by a relative error of at most 0.015.
Values may be sent and summed in bfloat16 or wider, within the bound.
A program may use at most 128 MiB of HBM per device.

```python
import jax
import jax.numpy as jnp
from jax import lax

C = 512
D = 1024
FF = 4096
FR = 2048
SLOT = 256
ROWS = 16384
N_DP = 8
N_MP = 4


def packing_plan(key):
    key_order, key_count, key_full = jax.random.split(jax.random.fold_in(key, 11), 3)
    orders = jax.vmap(lambda item: jax.random.permutation(item, FR))(jax.random.split(key_order, N_DP))
    counts = jax.random.randint(key_count, (N_DP,), FR // 4, FR + 1)
    full_sender = jax.random.randint(key_full, (), 0, N_DP)
    counts = jnp.where(jnp.arange(N_DP) == full_sender, FR, counts)
    return (orders.astype(jnp.int32), counts.astype(jnp.int32))


def draw_send_index(key, part):
    orders, counts = packing_plan(key)
    return orders.reshape(N_DP * FR).astype(jnp.int32)


def draw_slot_valid(key, part):
    orders, counts = packing_plan(key)
    inside = (orders < counts[:, None]).astype(jnp.int32)
    return jnp.transpose(inside.reshape(N_DP, N_DP, SLOT), (1, 0, 2)).reshape(N_DP * FR).astype(jnp.int32)


def spiked(drawn, own_key, source, target, blocks, factor):
    owner, partner = [(jnp.arange(drawn.shape[dim]) // (drawn.shape[dim] // blocks)).reshape([-1 if axis == dim else 1 for axis in range(drawn.ndim)]) for dim in (source, target)]
    chosen = jax.random.permutation(own_key, blocks)[partner]
    strong = (owner == chosen) | (owner == (partner + blocks // 2) % blocks)
    return jnp.where(strong, factor * drawn, drawn)


def level_of(key, shape, cuts, least, largest):
    def one(axis_at, parts):
        draws = jax.random.uniform(jax.random.fold_in(jax.random.fold_in(key, 6), axis_at), (parts,), jnp.float32, least / len(cuts), largest / len(cuts))
        return jnp.repeat(jnp.exp(draws), shape[axis_at] // parts).reshape((-1,) + (1,) * (len(shape) - axis_at - 1))

    level = one(*cuts[0])
    for cut in cuts[1:]:
        level = level * one(*cut)
    return level


def normal_values(own_key, extent, scale, most, cuts=(), kind=jnp.bfloat16):
    array = scale * jax.random.normal(own_key, extent, jnp.float32)
    if cuts:
        array = array * level_of(own_key, extent, cuts, -0.22, 0.18)
    return jnp.clip(array, -most, most).astype(kind)


def bell_draw_with(own_key, dims, spread, most, cuts, heavy, kind=jnp.bfloat16):
    result = spread * jax.random.normal(own_key, dims, jnp.float32)
    if cuts:
        result = result * level_of(own_key, dims, cuts, -0.22, 0.18)
    return jnp.clip(spiked(result, jax.random.fold_in(own_key, 3), *heavy), -most, most).astype(kind)


def setup_inputs(seed: int = 0) -> dict:
    streams_of = jax.random.split(jax.random.key(seed), 11)
    conv_in = normal_values(streams_of[0], (ROWS, 2 * C), 1.0, 6.0, ((0, 8),))
    conv_weight = normal_values(streams_of[1], (2 * C, C), (2 * C) ** -0.5, 0.1875, ((1, 4),))
    feature_gain = jnp.clip(1.0 + 0.18 * jax.random.normal(streams_of[2], (C,), jnp.float32), 0.1, 1.9)
    proj_weight = normal_values(streams_of[3], (C, D), C ** -0.5, 0.25)
    block_gain = jnp.clip(1.0 + 0.18 * jax.random.normal(streams_of[4], (D,), jnp.float32), 0.1, 1.9)
    w_in = normal_values(streams_of[5], (D, FF), D ** -0.5, 0.1875, ((1, 4),))
    w_out = normal_values(streams_of[6], (D, FF), FF ** -0.5, 0.09375, ((1, 4),))
    cotangent = bell_draw_with(streams_of[7], (ROWS, D), ((FR * N_DP) ** -0.5), 0.0625, ((0, 8),), (0, 1, 8, 2.0))
    send_index = draw_send_index(jax.random.fold_in(streams_of[10], 71), 0)
    slot_valid = draw_slot_valid(jax.random.fold_in(streams_of[10], 71), 0)
    return dict(conv_in=conv_in, conv_weight=conv_weight, feature_gain=feature_gain, proj_weight=proj_weight, block_gain=block_gain, w_in=w_in, w_out=w_out, cotangent=cotangent, send_index=send_index, slot_valid=slot_valid)


EPSILON = 1e-05
SQRT_HALF = 0.7071067811865476
INV_SQRT_TWO_PI = 0.3989422804014327

def gelu_exact(values):
    return 0.5 * values * (1.0 + lax.erf(values * SQRT_HALF))

def gelu_slope(values):
    return 0.5 * (1.0 + lax.erf(values * SQRT_HALF)) + values * INV_SQRT_TWO_PI * jnp.exp(-0.5 * values * values)

def normalize(values):
    row_mean = lax.optimization_barrier(jnp.mean(values, axis=-1, keepdims=True))
    centred = values - row_mean
    inv_std = lax.rsqrt(lax.optimization_barrier(jnp.mean(centred * centred, axis=-1, keepdims=True)) + EPSILON)
    return (centred * inv_std, inv_std)

def norm_back(upstream, normed, inv_std, gain_row):
    scaled = upstream * gain_row
    first_mean = lax.optimization_barrier(jnp.mean(scaled, axis=-1, keepdims=True))
    second_mean = lax.optimization_barrier(jnp.mean(scaled * normed, axis=-1, keepdims=True))
    return inv_std * (scaled - first_mean - normed * second_mean)

def contract_rows(left, right):
    return lax.dot_general(left, right, (((0,), (0,)), ((), ())), preferred_element_type=jnp.float32)

def contract_cols(left, right):
    return lax.dot_general(left, right, (((1,), (1,)), ((), ())), preferred_element_type=jnp.float32)

def reference(conv_in, conv_weight, feature_gain, proj_weight, block_gain, w_in, w_out, cotangent, send_index, slot_valid):
    pre_act = jnp.dot(conv_in, conv_weight, preferred_element_type=jnp.float32)
    features = gelu_exact(pre_act).astype(jnp.bfloat16)
    offsets = (jnp.arange(N_DP, dtype=jnp.int32) * FR).astype(jnp.int32)
    source = send_index.reshape(N_DP, N_DP, SLOT) + offsets[:, None, None]
    source = jnp.transpose(source, (1, 0, 2)).reshape(N_DP * FR).astype(jnp.int32)
    packed = features[source]
    slot_keep = slot_valid.astype(jnp.bfloat16)[:, None]
    block_width = FF // N_MP
    gain_feat = feature_gain.astype(jnp.float32)
    gain_block = block_gain.astype(jnp.float32)

    def group_step(totals, inputs):
        feat_rows, cot_rows, keep_rows = inputs
        feat_norm, feat_inv = normalize(feat_rows.astype(jnp.float32))
        feat_ln = (feat_norm * gain_feat).astype(jnp.bfloat16)
        hidden = jnp.dot(feat_ln, proj_weight, preferred_element_type=jnp.float32)
        hid_norm, hid_inv = normalize(hidden)
        hid_ln = (hid_norm * gain_block).astype(jnp.bfloat16)
        upward = jnp.dot(hid_ln, w_in, preferred_element_type=jnp.float32)
        active = gelu_exact(upward).astype(jnp.bfloat16)
        masked_cot = cot_rows * keep_rows
        grad_active = jnp.dot(masked_cot, w_out, preferred_element_type=jnp.float32)
        grad_upward = (grad_active * gelu_slope(upward)).astype(jnp.bfloat16)
        out_term = contract_rows(masked_cot, active)
        in_term = contract_rows(hid_ln, grad_upward)
        grad_normed = jnp.zeros(hidden.shape, jnp.float32)
        for block in range(N_MP):
            piece = contract_cols(grad_upward[:, block * block_width:(block + 1) * block_width], w_in[:, block * block_width:(block + 1) * block_width])
            rounded = lax.optimization_barrier(piece.astype(jnp.bfloat16))
            grad_normed = grad_normed + rounded.astype(jnp.float32)
        grad_hidden = (masked_cot.astype(jnp.float32) + norm_back(grad_normed, hid_norm, hid_inv, gain_block)).astype(jnp.bfloat16)
        proj_term = contract_rows(feat_ln, grad_hidden)
        grad_feat_ln = contract_cols(grad_hidden, proj_weight)
        grad_packed = norm_back(grad_feat_ln, feat_norm, feat_inv, gain_feat).astype(jnp.bfloat16)
        return ((totals[0] + proj_term, totals[1] + in_term, totals[2] + out_term), grad_packed)
    start = (jnp.zeros((C, D), jnp.float32), jnp.zeros((D, FF), jnp.float32), jnp.zeros((D, FF), jnp.float32))
    sums, grad_groups = lax.scan(group_step, start, (packed.reshape(N_DP, FR, C), cotangent.reshape(N_DP, FR, D), slot_keep.reshape(N_DP, FR, 1)))
    grad_proj_weight, grad_w_in, grad_w_out = sums
    grad_features = jnp.zeros((N_DP * FR, C), jnp.float32).at[source].add(grad_groups.reshape(N_DP * FR, C).astype(jnp.float32))
    grad_pre = (grad_features * gelu_slope(pre_act)).astype(jnp.bfloat16)
    grad_conv_weight = contract_rows(conv_in, grad_pre)
    return (grad_conv_weight, grad_proj_weight, grad_w_in, grad_w_out)
```

```python
import functools

import jax
import jax.numpy as jnp
from jax import lax
from jax.experimental import pallas as pl
from jax.experimental.pallas import tpu as pltpu
from jax.sharding import PartitionSpec as P

EPSILON = 1e-05
SQRT_HALF = 0.7071067811865476
INV_SQRT_TWO_PI = 0.3989422804014327
VMEM_LIMIT = 48 * 1024 * 1024


def gelu_exact(values):
    return 0.5 * values * (1.0 + lax.erf(values * SQRT_HALF))


def gelu_slope(values):
    return 0.5 * (1.0 + lax.erf(values * SQRT_HALF)) + values * INV_SQRT_TWO_PI * jnp.exp(
        -0.5 * values * values
    )


def normalize(values):
    row_mean = jnp.mean(values, axis=-1, keepdims=True)
    centred = values - row_mean
    inv_std = lax.rsqrt(jnp.mean(centred * centred, axis=-1, keepdims=True) + EPSILON)
    return (centred * inv_std, inv_std)


def norm_back(upstream, normed, inv_std, gain_row):
    scaled = upstream * gain_row
    first_mean = jnp.mean(scaled, axis=-1, keepdims=True)
    second_mean = jnp.mean(scaled * normed, axis=-1, keepdims=True)
    return inv_std * (scaled - first_mean - normed * second_mean)


def contract_rows(left, right):
    return lax.dot_general(
        left, right, (((0,), (0,)), ((), ())), preferred_element_type=jnp.float32
    )


def contract_cols(left, right):
    return lax.dot_general(
        left, right, (((1,), (1,)), ((), ())), preferred_element_type=jnp.float32
    )


def scatter_sum_kernel(parts, count, *refs):
    ins, outs = refs[:count], refs[count : 2 * count]
    first_in, staged, second_in = (refs[(2 + i) * count : (3 + i) * count] for i in range(3))
    send_one, recv_one, send_two, recv_two = refs[5 * count :]
    half = parts // 2
    me = lax.axis_index("dp")
    parity = lax.rem(me, 2)
    place = me // 2
    partner = me + 1 - 2 * parity
    order = list(range(1, half)) + [0]

    barrier = pltpu.get_barrier_semaphore()
    pl.semaphore_signal(
        barrier, inc=1, device_id={"dp": partner}, device_id_type=pl.DeviceIdType.MESH
    )
    for k in range(1, half):
        peer = 2 * lax.rem(place + k, half) + parity
        pl.semaphore_signal(
            barrier, inc=1, device_id={"dp": peer}, device_id_type=pl.DeviceIdType.MESH
        )
    pl.semaphore_wait(barrier, half)

    def each_tile(rows, body):
        def step(i, carry):
            body(pl.ds(pl.multiple_of(i * 16, 16), 16), i)
            return carry

        lax.fori_loop(0, rows // 16, step, 0)

    ones, twos = {}, {}
    for k in order:
        target = lax.rem(place + k, half)
        for i in range(count):
            rows = outs[i].shape[0]
            start = pl.multiple_of((2 * target + 1 - parity) * rows, rows)
            ones[k, i] = pltpu.make_async_remote_copy(
                src_ref=ins[i].at[pl.ds(start, rows)],
                dst_ref=first_in[i].at[k],
                send_sem=send_one.at[i, k],
                recv_sem=recv_one.at[i, k],
                device_id={"dp": partner},
                device_id_type=pl.DeviceIdType.MESH,
            )
            ones[k, i].start()
    for k in order:
        target = lax.rem(place + k, half)
        for i in range(count):
            rows = outs[i].shape[0]
            base = (2 * target + parity) * rows
            ones[k, i].wait_recv()

            def add(tile, step, i=i, k=k, base=base):
                mine = ins[i][pl.ds(pl.multiple_of(base + step * 16, 16), 16), :]
                total = mine.astype(jnp.float32) + first_in[i][k, tile, :].astype(jnp.float32)
                if k:
                    staged[i][k, tile, :] = total.astype(jnp.bfloat16)
                else:
                    outs[i][tile, :] = total

            each_tile(rows, add)
            if k:
                twos[k, i] = pltpu.make_async_remote_copy(
                    src_ref=staged[i].at[k],
                    dst_ref=second_in[i].at[k],
                    send_sem=send_two.at[i, k],
                    recv_sem=recv_two.at[i, k],
                    device_id={"dp": 2 * target + parity},
                    device_id_type=pl.DeviceIdType.MESH,
                )
                twos[k, i].start()
    for i in range(count):
        for k in range(1, half):
            twos[k, i].wait_recv()

        def gather(tile, step, i=i):
            total = outs[i][tile, :]
            for k in range(1, half):
                total = total + second_in[i][k, tile, :].astype(jnp.float32)
            outs[i][tile, :] = total

        each_tile(outs[i].shape[0], gather)
    for copy in list(ones.values()) + list(twos.values()):
        copy.wait_send()


def scatter_sum(terms, collective_id):
    parts = lax.axis_size("dp")
    half = parts // 2
    count = len(terms)
    blocks = [(term.shape[0] // parts, term.shape[1]) for term in terms]
    slots = [pltpu.VMEM((half,) + block, jnp.bfloat16) for block in blocks]
    sent = sum(term.size * 2 for term in terms)
    return pl.pallas_call(
        functools.partial(scatter_sum_kernel, parts, count),
        out_shape=[jax.ShapeDtypeStruct(block, jnp.float32) for block in blocks],
        in_specs=[pl.BlockSpec(memory_space=pltpu.VMEM)] * count,
        out_specs=[pl.BlockSpec(memory_space=pltpu.VMEM)] * count,
        scratch_shapes=slots * 3 + [pltpu.SemaphoreType.DMA((count, half))] * 4,
        compiler_params=pltpu.CompilerParams(
            collective_id=collective_id, has_side_effects=True, vmem_limit_bytes=VMEM_LIMIT
        ),
        cost_estimate=pl.CostEstimate(
            flops=sent * 4000, bytes_accessed=sent * 40, transcendentals=0
        ),
        name="scatter_sum",
    )(*terms)


def on_device(
    conv_in,
    conv_weight,
    feature_gain,
    proj_weight,
    block_gain,
    w_in,
    w_out,
    cotangent,
    send_index,
    slot_valid,
):
    frames = conv_in.shape[0]
    shards = lax.axis_size("mp")
    member = lax.axis_index("mp")
    pre_act = jnp.dot(conv_in, conv_weight, preferred_element_type=jnp.float32)
    features = gelu_exact(pre_act).astype(jnp.bfloat16)
    choose = (send_index[:, None] == jnp.arange(frames, dtype=send_index.dtype)).astype(jnp.bfloat16)
    outgoing = jnp.dot(choose, features, preferred_element_type=jnp.float32).astype(jnp.bfloat16)
    arrived = lax.all_to_all(outgoing, "dp", split_axis=0, concat_axis=0, tiled=True)
    packed = lax.all_gather(arrived, "mp", axis=1, tiled=True)
    feat_norm, feat_inv = normalize(packed.astype(jnp.float32))
    feat_ln = (feat_norm * feature_gain).astype(jnp.bfloat16)
    hidden = jnp.dot(feat_ln, proj_weight, preferred_element_type=jnp.float32)
    hid_norm, hid_inv = normalize(hidden)
    hid_ln = (hid_norm * block_gain).astype(jnp.bfloat16)
    upward = jnp.dot(hid_ln, w_in, preferred_element_type=jnp.float32)
    active = gelu_exact(upward).astype(jnp.bfloat16)
    masked_cot = cotangent * slot_valid.astype(jnp.bfloat16)[:, None]
    grad_active = jnp.dot(masked_cot, w_out, preferred_element_type=jnp.float32)
    grad_upward = (grad_active * gelu_slope(upward)).astype(jnp.bfloat16)
    out_term = contract_rows(masked_cot, active)
    in_term = contract_rows(hid_ln, grad_upward)
    partial_value = contract_cols(grad_upward, w_in)
    share_rows = frames // shards
    first_row = member * share_rows
    share_normed = lax.psum_scatter(
        partial_value.astype(jnp.bfloat16), "mp", scatter_dimension=0, tiled=True
    ).astype(jnp.float32)
    in_grad, out_grad = scatter_sum(
        [in_term.astype(jnp.bfloat16), out_term.astype(jnp.bfloat16)], 1
    )
    share_normed, in_grad, out_grad = lax.optimization_barrier((share_normed, in_grad, out_grad))
    share_cot = lax.dynamic_slice_in_dim(masked_cot, first_row, share_rows, 0).astype(jnp.float32)
    share_norm = lax.dynamic_slice_in_dim(hid_norm, first_row, share_rows, 0)
    share_inv = lax.dynamic_slice_in_dim(hid_inv, first_row, share_rows, 0)
    share_grad = (share_cot + norm_back(share_normed, share_norm, share_inv, block_gain)).astype(
        jnp.bfloat16
    )
    share_feat = lax.dynamic_slice_in_dim(feat_ln, first_row, share_rows, 0)
    share_feat_norm = lax.dynamic_slice_in_dim(feat_norm, first_row, share_rows, 0)
    share_feat_inv = lax.dynamic_slice_in_dim(feat_inv, first_row, share_rows, 0)
    grad_feat_ln = contract_cols(share_grad, proj_weight)
    grad_packed = norm_back(grad_feat_ln, share_feat_norm, share_feat_inv, feature_gain).astype(
        jnp.bfloat16
    )
    proj_term = contract_rows(share_feat, share_grad)
    proj_part = lax.psum_scatter(
        proj_term.astype(jnp.bfloat16), "mp", scatter_dimension=1, tiled=True
    )
    grad_mine = lax.all_to_all(grad_packed, "mp", split_axis=1, concat_axis=0, tiled=True)
    returned = lax.all_to_all(grad_mine, "dp", split_axis=0, concat_axis=0, tiled=True)
    grad_features = contract_rows(choose, returned)
    grad_pre = (grad_features * gelu_slope(pre_act)).astype(jnp.bfloat16)
    conv_term = contract_rows(conv_in, grad_pre)
    conv_grad, proj_grad = scatter_sum([conv_term.astype(jnp.bfloat16), proj_part], 2)
    grads = (conv_grad, proj_grad, in_grad, out_grad)
    result = (grads[0], grads[1], grads[2], grads[3])
    return result


def solution(mesh):
    placed = (
        P("dp", None),
        P(None, "mp"),
        P(),
        P(),
        P(),
        P(None, "mp"),
        P(None, "mp"),
        P("dp", None),
        P("dp"),
        P("dp"),
    )
    return jax.shard_map(
        on_device,
        mesh=mesh,
        in_specs=placed,
        out_specs=(P("dp", "mp"), P("dp", "mp"), P("dp", "mp"), P("dp", "mp")),
        check_vma=False,
    )
```

```python
import functools

import jax
import jax.numpy as jnp
from jax import lax
from jax.experimental import pallas as pl
from jax.experimental.pallas import tpu as pltpu
from jax.sharding import PartitionSpec as P

EPSILON = 1e-05
SQRT_HALF = 0.7071067811865476
INV_SQRT_TWO_PI = 0.3989422804014327
VMEM_LIMIT = 48 * 1024 * 1024


def gelu_exact(values):
    return 0.5 * values * (1.0 + lax.erf(values * SQRT_HALF))


def gelu_slope(values):
    return 0.5 * (1.0 + lax.erf(values * SQRT_HALF)) + values * INV_SQRT_TWO_PI * jnp.exp(
        -0.5 * values * values
    )


def normalize(values):
    row_mean = jnp.mean(values, axis=-1, keepdims=True)
    centred = values - row_mean
    inv_std = lax.rsqrt(jnp.mean(centred * centred, axis=-1, keepdims=True) + EPSILON)
    return (centred * inv_std, inv_std)


def norm_back(upstream, normed, inv_std, gain_row):
    scaled = upstream * gain_row
    first_mean = jnp.mean(scaled, axis=-1, keepdims=True)
    second_mean = jnp.mean(scaled * normed, axis=-1, keepdims=True)
    return inv_std * (scaled - first_mean - normed * second_mean)


def contract_rows(left, right):
    return lax.dot_general(
        left, right, (((0,), (0,)), ((), ())), preferred_element_type=jnp.float32
    )


def contract_cols(left, right):
    return lax.dot_general(
        left, right, (((1,), (1,)), ((), ())), preferred_element_type=jnp.float32
    )


def scatter_sum_kernel(parts, count, *refs):
    ins, outs = refs[:count], refs[count : 2 * count]
    first_in, staged, second_in = (refs[(2 + i) * count : (3 + i) * count] for i in range(3))
    send_one, recv_one, send_two, recv_two = refs[5 * count :]
    half = parts // 2
    me = lax.axis_index("dp")
    parity = lax.rem(me, 2)
    place = me // 2
    partner = me + 1 - 2 * parity
    order = list(range(1, half)) + [0]

    barrier = pltpu.get_barrier_semaphore()
    pl.semaphore_signal(
        barrier, inc=1, device_id={"dp": partner}, device_id_type=pl.DeviceIdType.MESH
    )
    for k in range(1, half):
        peer = 2 * lax.rem(place + k, half) + parity
        pl.semaphore_signal(
            barrier, inc=1, device_id={"dp": peer}, device_id_type=pl.DeviceIdType.MESH
        )
    pl.semaphore_wait(barrier, half)

    def each_tile(rows, body):
        def step(i, carry):
            body(pl.ds(pl.multiple_of(i * 16, 16), 16), i)
            return carry

        lax.fori_loop(0, rows // 16, step, 0)

    ones, twos = {}, {}
    for k in order:
        target = lax.rem(place + k, half)
        for i in range(count):
            rows = outs[i].shape[0]
            start = pl.multiple_of((2 * target + 1 - parity) * rows, rows)
            ones[k, i] = pltpu.make_async_remote_copy(
                src_ref=ins[i].at[pl.ds(start, rows)],
                dst_ref=first_in[i].at[k],
                send_sem=send_one.at[i, k],
                recv_sem=recv_one.at[i, k],
                device_id={"dp": partner},
                device_id_type=pl.DeviceIdType.MESH,
            )
            ones[k, i].start()
    for k in order:
        target = lax.rem(place + k, half)
        for i in range(count):
            rows = outs[i].shape[0]
            base = (2 * target + parity) * rows
            ones[k, i].wait_recv()

            def add(tile, step, i=i, k=k, base=base):
                mine = ins[i][pl.ds(pl.multiple_of(base + step * 16, 16), 16), :]
                total = mine.astype(jnp.float32) + first_in[i][k, tile, :].astype(jnp.float32)
                if k:
                    staged[i][k, tile, :] = total.astype(jnp.bfloat16)
                else:
                    outs[i][tile, :] = total

            each_tile(rows, add)
            if k:
                twos[k, i] = pltpu.make_async_remote_copy(
                    src_ref=staged[i].at[k],
                    dst_ref=second_in[i].at[k],
                    send_sem=send_two.at[i, k],
                    recv_sem=recv_two.at[i, k],
                    device_id={"dp": 2 * target + parity},
                    device_id_type=pl.DeviceIdType.MESH,
                )
                twos[k, i].start()
    for i in range(count):
        for k in range(1, half):
            twos[k, i].wait_recv()

        def gather(tile, step, i=i):
            total = outs[i][tile, :]
            for k in range(1, half):
                total = total + second_in[i][k, tile, :].astype(jnp.float32)
            outs[i][tile, :] = total

        each_tile(outs[i].shape[0], gather)
    for copy in list(ones.values()) + list(twos.values()):
        copy.wait_send()


def start_copy(src, dst, send_sem, recv_sem, axis, index):
    copy = pltpu.make_async_remote_copy(
        src_ref=src,
        dst_ref=dst,
        send_sem=send_sem,
        recv_sem=recv_sem,
        device_id={axis: index},
        device_id_type=pl.DeviceIdType.MESH,
    )
    copy.start()
    return copy


def greet(peers):
    barrier = pltpu.get_barrier_semaphore()
    for axis, index in peers:
        pl.semaphore_signal(
            barrier, inc=1, device_id={axis: index}, device_id_type=pl.DeviceIdType.MESH
        )
    pl.semaphore_wait(barrier, len(peers))


def block_of(index, size):
    return pl.ds(pl.multiple_of(index * size, size), size)


def forward_kernel(
    parts, shards, source, packed, arrived, dp_send, dp_recv, near_send, near_recv,
    far_send, far_recv, on_send, on_recv, local
):
    rows, width = source.shape[0] // parts, source.shape[1]
    d = lax.axis_index("dp")
    m = lax.axis_index("mp")
    near = m + 1 - 2 * lax.rem(m, 2)
    fars = shards // 2
    greet(
        [("dp", lax.rem(d + o, parts)) for o in range(1, parts)]
        + [("mp", near)]
        + [("mp", lax.rem(m + 2 * j, shards)) for j in range(1, fars)]
    )
    exchanged, passed, kept = [], [], []
    spans, far_copies = [], []
    for o in range(1, parts):
        target = lax.rem(d + o, parts)
        exchanged.append(
            start_copy(
                source.at[block_of(target, rows)],
                arrived.at[block_of(d, rows)],
                dp_send.at[o],
                dp_recv.at[o],
                "dp",
                target,
            )
        )

    def hand_on(o):
        for j in range(1, fars):
            far_copies[o][j - 1].wait_recv()
            col = block_of(lax.rem(m - 2 * j + shards, shards), width)
            piece = packed.at[spans[o], col]
            passed.append(
                start_copy(piece, piece, on_send.at[o, j], on_recv.at[o, j], "mp", near)
            )

    lag = 2
    nears = []
    for o in range(parts):
        span = block_of(lax.rem(d - o + parts, parts), rows)
        spans.append(span)
        if o:
            exchanged[o - 1].wait_recv()
        block = arrived.at[span] if o else source.at[span]
        mine = packed.at[span, block_of(m, width)]
        far_copies.append(
            [
                start_copy(
                    block, mine, far_send.at[o, j], far_recv.at[o, j], "mp",
                    lax.rem(m + 2 * j, shards),
                )
                for j in range(1, fars)
            ]
        )
        nears.append(start_copy(block, mine, near_send.at[o], near_recv.at[o], "mp", near))
        keep = pltpu.make_async_copy(block, mine, local.at[o])
        keep.start()
        kept.append(keep)
        if o >= lag:
            hand_on(o - lag)
    for o in range(parts - lag, parts):
        hand_on(o)
    for copy in nears + passed:
        copy.wait_recv()
    for copy in kept:
        copy.wait()
    for copy in exchanged + nears + passed + [c for group in far_copies for c in group]:
        copy.wait_send()


def forward_exchange(source, collective_id):
    parts, shards = lax.axis_size("dp"), lax.axis_size("mp")
    rows, width = source.shape
    fars = max(shards // 2, 1)
    return pl.pallas_call(
        functools.partial(forward_kernel, parts, shards),
        out_shape=jax.ShapeDtypeStruct((rows, width * shards), source.dtype),
        in_specs=[pl.BlockSpec(memory_space=pltpu.VMEM)],
        out_specs=pl.BlockSpec(memory_space=pltpu.VMEM),
        scratch_shapes=[pltpu.VMEM((rows, width), source.dtype)]
        + [pltpu.SemaphoreType.DMA((parts,))] * 4
        + [pltpu.SemaphoreType.DMA((parts, fars))] * 4
        + [pltpu.SemaphoreType.DMA((parts,))],
        compiler_params=pltpu.CompilerParams(
            collective_id=collective_id, has_side_effects=True, vmem_limit_bytes=VMEM_LIMIT
        ),
        name="forward_exchange",
    )(source)


def backward_kernel(
    parts, shards, grad, term, back, total_out, middle, first_in, staged, second_in,
    mp_send, mp_recv, dp_send, dp_recv, send_one, recv_one, send_two, recv_two, local
):
    share = grad.shape[0]
    rows, width = back.shape[0] // parts, back.shape[1]
    out_rows = total_out.shape[0]
    half = parts // 2
    d = lax.axis_index("dp")
    m = lax.axis_index("mp")
    parity = lax.rem(d, 2)
    place = d // 2
    partner = d + 1 - 2 * parity
    order = list(range(1, half)) + [0]
    greet(
        [("dp", lax.rem(d + o, parts)) for o in range(1, parts)]
        + [("mp", lax.rem(m + o, shards)) for o in range(1, shards)]
    )
    columns = []
    for o in range(1, shards):
        peer = lax.rem(m + o, shards)
        columns.append(
            start_copy(
                grad.at[:, block_of(peer, width)],
                middle.at[block_of(m, share)],
                mp_send.at[o],
                mp_recv.at[o],
                "mp",
                peer,
            )
        )
    own_column = pltpu.make_async_copy(
        grad.at[:, block_of(m, width)], middle.at[block_of(m, share)], local.at[0]
    )
    own_column.start()

    def pair(k):
        target = lax.rem(place + k, half)
        return start_copy(
            term.at[block_of(2 * target + 1 - parity, out_rows)],
            first_in.at[k],
            send_one.at[k],
            recv_one.at[k],
            "dp",
            partner,
        )

    ones = {order[0]: pair(order[0])}
    for copy in columns:
        copy.wait_recv()
    own_column.wait()
    blocks = []
    for o in range(1, parts):
        target = lax.rem(d + o, parts)
        blocks.append(
            start_copy(
                middle.at[block_of(target, rows)],
                back.at[block_of(d, rows)],
                dp_send.at[o],
                dp_recv.at[o],
                "dp",
                target,
            )
        )
    own_block = pltpu.make_async_copy(
        middle.at[block_of(d, rows)], back.at[block_of(d, rows)], local.at[1]
    )
    own_block.start()
    for k in order[1:]:
        ones[k] = pair(k)

    def each_tile(body):
        def step(i, carry):
            body(block_of(i, 16), i)
            return carry

        lax.fori_loop(0, out_rows // 16, step, 0)

    twos = []
    for k in order:
        target = lax.rem(place + k, half)
        base = (2 * target + parity) * out_rows
        ones[k].wait_recv()

        def add(tile, step, k=k, base=base):
            mine = term[pl.ds(pl.multiple_of(base + step * 16, 16), 16), :]
            total = mine.astype(jnp.float32) + first_in[k, tile, :].astype(jnp.float32)
            if k:
                staged[k, tile, :] = total.astype(jnp.bfloat16)
            else:
                total_out[tile, :] = total

        each_tile(add)
        if k:
            twos.append(
                start_copy(
                    staged.at[k],
                    second_in.at[k],
                    send_two.at[k],
                    recv_two.at[k],
                    "dp",
                    2 * target + parity,
                )
            )
    for copy in twos:
        copy.wait_recv()

    def gather(tile, step):
        total = total_out[tile, :]
        for k in range(1, half):
            total = total + second_in[k, tile, :].astype(jnp.float32)
        total_out[tile, :] = total

    each_tile(gather)
    for copy in blocks:
        copy.wait_recv()
    own_block.wait()
    for copy in columns + blocks + list(ones.values()) + twos:
        copy.wait_send()


def backward_exchange(grad, term, collective_id):
    parts, shards = lax.axis_size("dp"), lax.axis_size("mp")
    half = parts // 2
    share, channels = grad.shape
    back = (share * shards, channels // shards)
    block = (term.shape[0] // parts, term.shape[1])
    slots = pltpu.VMEM((half,) + block, jnp.bfloat16)
    return pl.pallas_call(
        functools.partial(backward_kernel, parts, shards),
        out_shape=[
            jax.ShapeDtypeStruct(back, grad.dtype),
            jax.ShapeDtypeStruct(block, jnp.float32),
        ],
        in_specs=[pl.BlockSpec(memory_space=pltpu.VMEM)] * 2,
        out_specs=[pl.BlockSpec(memory_space=pltpu.VMEM)] * 2,
        scratch_shapes=[pltpu.VMEM(back, grad.dtype), slots, slots, slots]
        + [pltpu.SemaphoreType.DMA((shards,))] * 2
        + [pltpu.SemaphoreType.DMA((parts,))] * 2
        + [pltpu.SemaphoreType.DMA((half,))] * 4
        + [pltpu.SemaphoreType.DMA((2,))],
        compiler_params=pltpu.CompilerParams(
            collective_id=collective_id, has_side_effects=True, vmem_limit_bytes=VMEM_LIMIT
        ),
        cost_estimate=pl.CostEstimate(
            flops=term.size * 8000, bytes_accessed=term.size * 80, transcendentals=0
        ),
        name="backward_exchange",
    )(grad, term)


def scatter_sum(terms, collective_id):
    parts = lax.axis_size("dp")
    half = parts // 2
    count = len(terms)
    blocks = [(term.shape[0] // parts, term.shape[1]) for term in terms]
    slots = [pltpu.VMEM((half,) + block, jnp.bfloat16) for block in blocks]
    sent = sum(term.size * 2 for term in terms)
    return pl.pallas_call(
        functools.partial(scatter_sum_kernel, parts, count),
        out_shape=[jax.ShapeDtypeStruct(block, jnp.float32) for block in blocks],
        in_specs=[pl.BlockSpec(memory_space=pltpu.VMEM)] * count,
        out_specs=[pl.BlockSpec(memory_space=pltpu.VMEM)] * count,
        scratch_shapes=slots * 3 + [pltpu.SemaphoreType.DMA((count, half))] * 4,
        compiler_params=pltpu.CompilerParams(
            collective_id=collective_id, has_side_effects=True, vmem_limit_bytes=VMEM_LIMIT
        ),
        cost_estimate=pl.CostEstimate(
            flops=sent * 4000, bytes_accessed=sent * 40, transcendentals=0
        ),
        name="scatter_sum",
    )(*terms)


def on_device(
    conv_in,
    conv_weight,
    feature_gain,
    proj_weight,
    block_gain,
    w_in,
    w_out,
    cotangent,
    send_index,
    slot_valid,
):
    frames = conv_in.shape[0]
    shards = lax.axis_size("mp")
    member = lax.axis_index("mp")
    pre_act = jnp.dot(conv_in, conv_weight, preferred_element_type=jnp.float32)
    features = gelu_exact(pre_act).astype(jnp.bfloat16)
    choose = (send_index[:, None] == jnp.arange(frames, dtype=send_index.dtype)).astype(jnp.bfloat16)
    outgoing = jnp.dot(choose, features, preferred_element_type=jnp.float32).astype(jnp.bfloat16)
    packed = forward_exchange(outgoing, 3)
    feat_norm, feat_inv = normalize(packed.astype(jnp.float32))
    feat_ln = (feat_norm * feature_gain).astype(jnp.bfloat16)
    hidden = jnp.dot(feat_ln, proj_weight, preferred_element_type=jnp.float32)
    hid_norm, hid_inv = normalize(hidden)
    hid_ln = (hid_norm * block_gain).astype(jnp.bfloat16)
    upward = jnp.dot(hid_ln, w_in, preferred_element_type=jnp.float32)
    valid = slot_valid.astype(jnp.float32)[:, None]
    active = (valid * gelu_exact(upward)).astype(jnp.bfloat16)
    grad_active = valid * jnp.dot(cotangent, w_out, preferred_element_type=jnp.float32)
    grad_upward = (grad_active * gelu_slope(upward)).astype(jnp.bfloat16)
    out_term = contract_rows(cotangent, active)
    in_term = contract_rows(hid_ln, grad_upward)
    partial_value = contract_cols(grad_upward, w_in)
    share_rows = frames // shards
    first_row = member * share_rows
    share_normed = lax.psum_scatter(
        partial_value.astype(jnp.bfloat16), "mp", scatter_dimension=0, tiled=True
    ).astype(jnp.float32)
    in_term = in_term.astype(jnp.bfloat16)
    (out_grad,) = scatter_sum([out_term.astype(jnp.bfloat16)], 1)
    share_normed, in_term, out_grad = lax.optimization_barrier((share_normed, in_term, out_grad))
    share_cot = lax.dynamic_slice_in_dim(valid, first_row, share_rows, 0) * (
        lax.dynamic_slice_in_dim(cotangent, first_row, share_rows, 0).astype(jnp.float32)
    )
    share_norm = lax.dynamic_slice_in_dim(hid_norm, first_row, share_rows, 0)
    share_inv = lax.dynamic_slice_in_dim(hid_inv, first_row, share_rows, 0)
    share_grad = (share_cot + norm_back(share_normed, share_norm, share_inv, block_gain)).astype(
        jnp.bfloat16
    )
    share_feat = lax.dynamic_slice_in_dim(feat_ln, first_row, share_rows, 0)
    share_feat_norm = lax.dynamic_slice_in_dim(feat_norm, first_row, share_rows, 0)
    share_feat_inv = lax.dynamic_slice_in_dim(feat_inv, first_row, share_rows, 0)
    grad_feat_ln = contract_cols(share_grad, proj_weight)
    grad_packed = norm_back(grad_feat_ln, share_feat_norm, share_feat_inv, feature_gain).astype(
        jnp.bfloat16
    )
    proj_term = contract_rows(share_feat, share_grad)
    proj_part = lax.psum_scatter(
        proj_term.astype(jnp.bfloat16), "mp", scatter_dimension=1, tiled=True
    )
    returned, in_grad = backward_exchange(grad_packed, in_term, 4)
    grad_features = contract_rows(choose, returned)
    grad_pre = (grad_features * gelu_slope(pre_act)).astype(jnp.bfloat16)
    conv_term = contract_rows(conv_in, grad_pre)
    conv_grad, proj_grad = scatter_sum([conv_term.astype(jnp.bfloat16), proj_part], 2)
    grads = (conv_grad, proj_grad, in_grad, out_grad)
    result = (grads[0], grads[1], grads[2], grads[3])
    return result


def solution(mesh):
    placed = (
        P("dp", None),
        P(None, "mp"),
        P(),
        P(),
        P(),
        P(None, "mp"),
        P(None, "mp"),
        P("dp", None),
        P("dp"),
        P("dp"),
    )
    return jax.shard_map(
        on_device,
        mesh=mesh,
        in_specs=placed,
        out_specs=(P("dp", "mp"), P("dp", "mp"), P("dp", "mp"), P("dp", "mp")),
        check_vma=False,
    )
```

```python
import functools

import jax
import jax.numpy as jnp
from jax import lax
from jax.experimental import pallas as pl
from jax.experimental.pallas import tpu as pltpu
from jax.sharding import PartitionSpec as P

EPSILON = 1e-05
SQRT_HALF = 0.7071067811865476
INV_SQRT_TWO_PI = 0.3989422804014327
VMEM_LIMIT = 48 * 1024 * 1024


def gelu_exact(values):
    return 0.5 * values * (1.0 + lax.erf(values * SQRT_HALF))


def gelu_slope(values):
    return 0.5 * (1.0 + lax.erf(values * SQRT_HALF)) + values * INV_SQRT_TWO_PI * jnp.exp(
        -0.5 * values * values
    )


def normalize(values):
    row_mean = jnp.mean(values, axis=-1, keepdims=True)
    centred = values - row_mean
    inv_std = lax.rsqrt(jnp.mean(centred * centred, axis=-1, keepdims=True) + EPSILON)
    return (centred * inv_std, inv_std)


def norm_back(upstream, normed, inv_std, gain_row):
    scaled = upstream * gain_row
    first_mean = jnp.mean(scaled, axis=-1, keepdims=True)
    second_mean = jnp.mean(scaled * normed, axis=-1, keepdims=True)
    return inv_std * (scaled - first_mean - normed * second_mean)


def contract_rows(left, right):
    return lax.dot_general(
        left, right, (((0,), (0,)), ((), ())), preferred_element_type=jnp.float32
    )


def contract_cols(left, right):
    return lax.dot_general(
        left, right, (((1,), (1,)), ((), ())), preferred_element_type=jnp.float32
    )


def scatter_sum_kernel(parts, count, *refs):
    ins, outs = refs[:count], refs[count : 2 * count]
    first_in, staged, second_in = (refs[(2 + i) * count : (3 + i) * count] for i in range(3))
    send_one, recv_one, send_two, recv_two = refs[5 * count :]
    half = parts // 2
    me = lax.axis_index("dp")
    parity = lax.rem(me, 2)
    place = me // 2
    partner = me + 1 - 2 * parity
    order = list(range(1, half)) + [0]

    barrier = pltpu.get_barrier_semaphore()
    pl.semaphore_signal(
        barrier, inc=1, device_id={"dp": partner}, device_id_type=pl.DeviceIdType.MESH
    )
    for k in range(1, half):
        peer = 2 * lax.rem(place + k, half) + parity
        pl.semaphore_signal(
            barrier, inc=1, device_id={"dp": peer}, device_id_type=pl.DeviceIdType.MESH
        )
    pl.semaphore_wait(barrier, half)

    def each_tile(rows, body):
        def step(i, carry):
            body(pl.ds(pl.multiple_of(i * 16, 16), 16), i)
            return carry

        lax.fori_loop(0, rows // 16, step, 0)

    ones, twos = {}, {}
    for k in order:
        target = lax.rem(place + k, half)
        for i in range(count):
            rows = outs[i].shape[0]
            start = pl.multiple_of((2 * target + 1 - parity) * rows, rows)
            ones[k, i] = pltpu.make_async_remote_copy(
                src_ref=ins[i].at[pl.ds(start, rows)],
                dst_ref=first_in[i].at[k],
                send_sem=send_one.at[i, k],
                recv_sem=recv_one.at[i, k],
                device_id={"dp": partner},
                device_id_type=pl.DeviceIdType.MESH,
            )
            ones[k, i].start()
    for k in order:
        target = lax.rem(place + k, half)
        for i in range(count):
            rows = outs[i].shape[0]
            base = (2 * target + parity) * rows
            ones[k, i].wait_recv()

            def add(tile, step, i=i, k=k, base=base):
                mine = ins[i][pl.ds(pl.multiple_of(base + step * 16, 16), 16), :]
                total = mine.astype(jnp.float32) + first_in[i][k, tile, :].astype(jnp.float32)
                if k:
                    staged[i][k, tile, :] = total.astype(jnp.bfloat16)
                else:
                    outs[i][tile, :] = total

            each_tile(rows, add)
            if k:
                twos[k, i] = pltpu.make_async_remote_copy(
                    src_ref=staged[i].at[k],
                    dst_ref=second_in[i].at[k],
                    send_sem=send_two.at[i, k],
                    recv_sem=recv_two.at[i, k],
                    device_id={"dp": 2 * target + parity},
                    device_id_type=pl.DeviceIdType.MESH,
                )
                twos[k, i].start()
    for i in range(count):
        for k in range(1, half):
            twos[k, i].wait_recv()

        def gather(tile, step, i=i):
            total = outs[i][tile, :]
            for k in range(1, half):
                total = total + second_in[i][k, tile, :].astype(jnp.float32)
            outs[i][tile, :] = total

        each_tile(outs[i].shape[0], gather)
    for copy in list(ones.values()) + list(twos.values()):
        copy.wait_send()


def start_copy(src, dst, send_sem, recv_sem, axis, index):
    copy = pltpu.make_async_remote_copy(
        src_ref=src,
        dst_ref=dst,
        send_sem=send_sem,
        recv_sem=recv_sem,
        device_id={axis: index},
        device_id_type=pl.DeviceIdType.MESH,
    )
    copy.start()
    return copy


def greet(peers):
    barrier = pltpu.get_barrier_semaphore()
    for axis, index in peers:
        pl.semaphore_signal(
            barrier, inc=1, device_id={axis: index}, device_id_type=pl.DeviceIdType.MESH
        )
    pl.semaphore_wait(barrier, len(peers))


def block_of(index, size):
    return pl.ds(pl.multiple_of(index * size, size), size)


def product_sum_kernel(parts, count, *refs):
    pairs = [(refs[2 * i], refs[2 * i + 1]) for i in range(count)]
    outs = refs[2 * count : 3 * count]
    made, first_in, staged, second_in = (
        refs[(3 + i) * count : (4 + i) * count] for i in range(4)
    )
    send_one, recv_one, send_two, recv_two = refs[7 * count :]
    half = parts // 2
    d = lax.axis_index("dp")
    parity = lax.rem(d, 2)
    place = d // 2
    partner = d + 1 - 2 * parity
    order = list(range(1, half)) + [0]
    greet(
        [("dp", partner)]
        + [("dp", 2 * lax.rem(place + k, half) + parity) for k in range(1, half)]
    )

    def make(i, index):
        left, right = pairs[i]
        rows = outs[i].shape[0]
        span = block_of(index, rows)
        if rows % 128 == 0:
            piece = left[:, block_of(index, rows)]
            made[i][span, :] = contract_rows(piece, right[...]).astype(jnp.bfloat16)

    def make_all(i):
        left, right = pairs[i]

        def step(t, carry):
            made[i][block_of(t, 128), :] = contract_rows(
                left[:, block_of(t, 128)], right[...]
            ).astype(jnp.bfloat16)
            return carry

        lax.fori_loop(0, left.shape[1] // 128, step, 0)

    def first(i, k):
        rows = outs[i].shape[0]
        target = lax.rem(place + k, half)
        return pltpu.make_async_remote_copy(
            src_ref=made[i].at[block_of(2 * target + 1 - parity, rows)],
            dst_ref=first_in[i].at[k],
            send_sem=send_one.at[i, k],
            recv_sem=recv_one.at[i, k],
            device_id={"dp": partner},
            device_id_type=pl.DeviceIdType.MESH,
        )

    for i in range(count):
        whole = outs[i].shape[0] % 128 != 0
        if whole:
            make_all(i)

        def send(t, carry, i=i, whole=whole):
            k = lax.rem(t + 1, half)
            if not whole:
                make(i, 2 * lax.rem(place + k, half) + 1 - parity)
            first(i, k).start()
            return carry

        lax.fori_loop(0, half, send, 0)

        def keep(t, carry, i=i):
            make(i, 2 * t + parity)
            return carry

        if not whole:
            lax.fori_loop(0, half, keep, 0)

    def each_tile(rows, body):
        def step(t, carry):
            body(block_of(t, 16), t)
            return carry

        lax.fori_loop(0, rows // 16, step, 0)

    twos = {}
    for i in range(count):
        for k in order:
            rows = outs[i].shape[0]
            target = lax.rem(place + k, half)
            base = (2 * target + parity) * rows
            first(i, k).wait_recv()

            def add(tile, step, i=i, k=k, base=base):
                mine = made[i][pl.ds(pl.multiple_of(base + step * 16, 16), 16), :]
                total = mine.astype(jnp.float32) + first_in[i][k, tile, :].astype(jnp.float32)
                if k:
                    staged[i][k, tile, :] = total.astype(jnp.bfloat16)
                else:
                    outs[i][tile, :] = total

            each_tile(rows, add)
            if k:
                twos[i, k] = start_copy(
                    staged[i].at[k],
                    second_in[i].at[k],
                    send_two.at[i, k],
                    recv_two.at[i, k],
                    "dp",
                    2 * target + parity,
                )
    for i in range(count):
        for k in range(1, half):
            twos[i, k].wait_recv()

        def gather(tile, step, i=i):
            total = outs[i][tile, :]
            for k in range(1, half):
                total = total + second_in[i][k, tile, :].astype(jnp.float32)
            outs[i][tile, :] = total

        each_tile(outs[i].shape[0], gather)
    for i in range(count):
        for k in range(half):
            first(i, k).wait_send()
    for copy in twos.values():
        copy.wait_send()


def product_sum(pairs, collective_id):
    parts = lax.axis_size("dp")
    half = parts // 2
    count = len(pairs)
    shapes = [(left.shape[1], right.shape[1]) for left, right in pairs]
    blocks = [(rows // parts, cols) for rows, cols in shapes]
    slots = [pltpu.VMEM((half,) + block, jnp.bfloat16) for block in blocks]
    sent = sum(rows * cols * 2 for rows, cols in shapes)
    return pl.pallas_call(
        functools.partial(product_sum_kernel, parts, count),
        out_shape=[jax.ShapeDtypeStruct(block, jnp.float32) for block in blocks],
        in_specs=[pl.BlockSpec(memory_space=pltpu.VMEM)] * (2 * count),
        out_specs=[pl.BlockSpec(memory_space=pltpu.VMEM)] * count,
        scratch_shapes=[pltpu.VMEM(shape, jnp.bfloat16) for shape in shapes]
        + slots * 3
        + [pltpu.SemaphoreType.DMA((count, half))] * 4,
        compiler_params=pltpu.CompilerParams(
            collective_id=collective_id, has_side_effects=True, vmem_limit_bytes=VMEM_LIMIT
        ),
        cost_estimate=pl.CostEstimate(
            flops=sent * 4000, bytes_accessed=sent * 40, transcendentals=0
        ),
        name="product_sum",
    )(*[value for pair in pairs for value in pair])


def forward_kernel(
    parts, shards, source, packed, arrived, dp_send, dp_recv, near_send, near_recv,
    far_send, far_recv, on_send, on_recv, local
):
    rows, width = source.shape[0] // parts, source.shape[1]
    d = lax.axis_index("dp")
    m = lax.axis_index("mp")
    near = m + 1 - 2 * lax.rem(m, 2)
    fars = shards // 2
    greet(
        [("dp", lax.rem(d + o, parts)) for o in range(1, parts)]
        + [("mp", near)]
        + [("mp", lax.rem(m + 2 * j, shards)) for j in range(1, fars)]
    )
    exchanged, passed, kept = [], [], []
    spans, far_copies = [], []
    for o in range(1, parts):
        target = lax.rem(d + o, parts)
        exchanged.append(
            start_copy(
                source.at[block_of(target, rows)],
                arrived.at[block_of(d, rows)],
                dp_send.at[o],
                dp_recv.at[o],
                "dp",
                target,
            )
        )

    def hand_on(o):
        for j in range(1, fars):
            far_copies[o][j - 1].wait_recv()
            col = block_of(lax.rem(m - 2 * j + shards, shards), width)
            piece = packed.at[spans[o], col]
            passed.append(
                start_copy(piece, piece, on_send.at[o, j], on_recv.at[o, j], "mp", near)
            )

    lag = 2
    nears = []
    for o in range(parts):
        span = block_of(lax.rem(d - o + parts, parts), rows)
        spans.append(span)
        if o:
            exchanged[o - 1].wait_recv()
        block = arrived.at[span] if o else source.at[span]
        mine = packed.at[span, block_of(m, width)]
        far_copies.append(
            [
                start_copy(
                    block, mine, far_send.at[o, j], far_recv.at[o, j], "mp",
                    lax.rem(m + 2 * j, shards),
                )
                for j in range(1, fars)
            ]
        )
        nears.append(start_copy(block, mine, near_send.at[o], near_recv.at[o], "mp", near))
        keep = pltpu.make_async_copy(block, mine, local.at[o])
        keep.start()
        kept.append(keep)
        if o >= lag:
            hand_on(o - lag)
    for o in range(parts - lag, parts):
        hand_on(o)
    for copy in nears + passed:
        copy.wait_recv()
    for copy in kept:
        copy.wait()
    for copy in exchanged + nears + passed + [c for group in far_copies for c in group]:
        copy.wait_send()


def forward_exchange(source, collective_id):
    parts, shards = lax.axis_size("dp"), lax.axis_size("mp")
    rows, width = source.shape
    fars = max(shards // 2, 1)
    return pl.pallas_call(
        functools.partial(forward_kernel, parts, shards),
        out_shape=jax.ShapeDtypeStruct((rows, width * shards), source.dtype),
        in_specs=[pl.BlockSpec(memory_space=pltpu.VMEM)],
        out_specs=pl.BlockSpec(memory_space=pltpu.VMEM),
        scratch_shapes=[pltpu.VMEM((rows, width), source.dtype)]
        + [pltpu.SemaphoreType.DMA((parts,))] * 4
        + [pltpu.SemaphoreType.DMA((parts, fars))] * 4
        + [pltpu.SemaphoreType.DMA((parts,))],
        compiler_params=pltpu.CompilerParams(
            collective_id=collective_id, has_side_effects=True, vmem_limit_bytes=VMEM_LIMIT
        ),
        name="forward_exchange",
    )(source)


def backward_kernel(
    parts, shards, grad, back, middle, mp_send, mp_recv, dp_send, dp_recv, local
):
    share = grad.shape[0]
    rows, width = back.shape[0] // parts, back.shape[1]
    d = lax.axis_index("dp")
    m = lax.axis_index("mp")
    greet(
        [("dp", lax.rem(d + o, parts)) for o in range(1, parts)]
        + [("mp", lax.rem(m + o, shards)) for o in range(1, shards)]
    )
    columns = []
    for o in range(1, shards):
        peer = lax.rem(m + o, shards)
        columns.append(
            start_copy(
                grad.at[:, block_of(peer, width)],
                middle.at[block_of(m, share)],
                mp_send.at[o],
                mp_recv.at[o],
                "mp",
                peer,
            )
        )
    own_column = pltpu.make_async_copy(
        grad.at[:, block_of(m, width)], middle.at[block_of(m, share)], local.at[0]
    )
    own_column.start()

    for copy in columns:
        copy.wait_recv()
    own_column.wait()
    blocks = []
    for o in range(1, parts):
        target = lax.rem(d + o, parts)
        blocks.append(
            start_copy(
                middle.at[block_of(target, rows)],
                back.at[block_of(d, rows)],
                dp_send.at[o],
                dp_recv.at[o],
                "dp",
                target,
            )
        )
    own_block = pltpu.make_async_copy(
        middle.at[block_of(d, rows)], back.at[block_of(d, rows)], local.at[1]
    )
    own_block.start()
    for copy in blocks:
        copy.wait_recv()
    own_block.wait()
    for copy in columns + blocks:
        copy.wait_send()


def backward_exchange(grad, collective_id):
    parts, shards = lax.axis_size("dp"), lax.axis_size("mp")
    share, channels = grad.shape
    back = (share * shards, channels // shards)
    return pl.pallas_call(
        functools.partial(backward_kernel, parts, shards),
        out_shape=jax.ShapeDtypeStruct(back, grad.dtype),
        in_specs=[pl.BlockSpec(memory_space=pltpu.VMEM)],
        out_specs=pl.BlockSpec(memory_space=pltpu.VMEM),
        scratch_shapes=[pltpu.VMEM(back, grad.dtype)]
        + [pltpu.SemaphoreType.DMA((shards,))] * 2
        + [pltpu.SemaphoreType.DMA((parts,))] * 2
        + [pltpu.SemaphoreType.DMA((2,))],
        compiler_params=pltpu.CompilerParams(
            collective_id=collective_id, has_side_effects=True, vmem_limit_bytes=VMEM_LIMIT
        ),
        name="backward_exchange",
    )(grad)


def scatter_sum(terms, collective_id):
    parts = lax.axis_size("dp")
    half = parts // 2
    count = len(terms)
    blocks = [(term.shape[0] // parts, term.shape[1]) for term in terms]
    slots = [pltpu.VMEM((half,) + block, jnp.bfloat16) for block in blocks]
    sent = sum(term.size * 2 for term in terms)
    return pl.pallas_call(
        functools.partial(scatter_sum_kernel, parts, count),
        out_shape=[jax.ShapeDtypeStruct(block, jnp.float32) for block in blocks],
        in_specs=[pl.BlockSpec(memory_space=pltpu.VMEM)] * count,
        out_specs=[pl.BlockSpec(memory_space=pltpu.VMEM)] * count,
        scratch_shapes=slots * 3 + [pltpu.SemaphoreType.DMA((count, half))] * 4,
        compiler_params=pltpu.CompilerParams(
            collective_id=collective_id, has_side_effects=True, vmem_limit_bytes=VMEM_LIMIT
        ),
        cost_estimate=pl.CostEstimate(
            flops=sent * 4000, bytes_accessed=sent * 40, transcendentals=0
        ),
        name="scatter_sum",
    )(*terms)


def on_device(
    conv_in,
    conv_weight,
    feature_gain,
    proj_weight,
    block_gain,
    w_in,
    w_out,
    cotangent,
    send_index,
    slot_valid,
):
    frames = conv_in.shape[0]
    shards = lax.axis_size("mp")
    member = lax.axis_index("mp")
    pre_act = jnp.dot(conv_in, conv_weight, preferred_element_type=jnp.float32)
    features = gelu_exact(pre_act).astype(jnp.bfloat16)
    choose = (send_index[:, None] == jnp.arange(frames, dtype=send_index.dtype)).astype(jnp.bfloat16)
    outgoing = jnp.dot(choose, features, preferred_element_type=jnp.float32).astype(jnp.bfloat16)
    packed = forward_exchange(outgoing, 3)
    feat_norm, feat_inv = normalize(packed.astype(jnp.float32))
    feat_ln = (feat_norm * feature_gain).astype(jnp.bfloat16)
    hidden = jnp.dot(feat_ln, proj_weight, preferred_element_type=jnp.float32)
    hid_norm, hid_inv = normalize(hidden)
    hid_ln = (hid_norm * block_gain).astype(jnp.bfloat16)
    upward = jnp.dot(hid_ln, w_in, preferred_element_type=jnp.float32)
    valid = slot_valid.astype(jnp.float32)[:, None]
    active = (valid * gelu_exact(upward)).astype(jnp.bfloat16)
    grad_active = valid * jnp.dot(cotangent, w_out, preferred_element_type=jnp.float32)
    grad_upward = (grad_active * gelu_slope(upward)).astype(jnp.bfloat16)
    partial_value = contract_cols(grad_upward, w_in)
    share_rows = frames // shards
    first_row = member * share_rows
    share_normed = lax.psum_scatter(
        partial_value.astype(jnp.bfloat16), "mp", scatter_dimension=0, tiled=True
    ).astype(jnp.float32)
    out_grad, in_grad = product_sum([(cotangent, active), (hid_ln, grad_upward)], 1)
    share_normed, in_grad, out_grad = lax.optimization_barrier((share_normed, in_grad, out_grad))
    share_cot = lax.dynamic_slice_in_dim(valid, first_row, share_rows, 0) * (
        lax.dynamic_slice_in_dim(cotangent, first_row, share_rows, 0).astype(jnp.float32)
    )
    share_norm = lax.dynamic_slice_in_dim(hid_norm, first_row, share_rows, 0)
    share_inv = lax.dynamic_slice_in_dim(hid_inv, first_row, share_rows, 0)
    share_grad = (share_cot + norm_back(share_normed, share_norm, share_inv, block_gain)).astype(
        jnp.bfloat16
    )
    share_feat = lax.dynamic_slice_in_dim(feat_ln, first_row, share_rows, 0)
    share_feat_norm = lax.dynamic_slice_in_dim(feat_norm, first_row, share_rows, 0)
    share_feat_inv = lax.dynamic_slice_in_dim(feat_inv, first_row, share_rows, 0)
    grad_feat_ln = contract_cols(share_grad, proj_weight)
    grad_packed = norm_back(grad_feat_ln, share_feat_norm, share_feat_inv, feature_gain).astype(
        jnp.bfloat16
    )
    proj_term = contract_rows(share_feat, share_grad)
    proj_part = lax.psum_scatter(
        proj_term.astype(jnp.bfloat16), "mp", scatter_dimension=1, tiled=True
    )
    returned = backward_exchange(grad_packed, 4)
    grad_features = contract_rows(choose, returned)
    grad_pre = (grad_features * gelu_slope(pre_act)).astype(jnp.bfloat16)
    conv_term = contract_rows(conv_in, grad_pre)
    conv_grad, proj_grad = scatter_sum([conv_term.astype(jnp.bfloat16), proj_part], 2)
    grads = (conv_grad, proj_grad, in_grad, out_grad)
    result = (grads[0], grads[1], grads[2], grads[3])
    return result


def solution(mesh):
    placed = (
        P("dp", None),
        P(None, "mp"),
        P(),
        P(),
        P(),
        P(None, "mp"),
        P(None, "mp"),
        P("dp", None),
        P("dp"),
        P("dp"),
    )
    return jax.shard_map(
        on_device,
        mesh=mesh,
        in_specs=placed,
        out_specs=(P("dp", "mp"), P("dp", "mp"), P("dp", "mp"), P("dp", "mp")),
        check_vma=False,
    )
```

```python
import functools

import jax
import jax.numpy as jnp
from jax import lax
from jax.experimental import pallas as pl
from jax.experimental.pallas import tpu as pltpu
from jax.sharding import PartitionSpec as P

EPSILON = 1e-05
SQRT_HALF = 0.7071067811865476
INV_SQRT_TWO_PI = 0.3989422804014327
VMEM_LIMIT = 48 * 1024 * 1024


def gelu_exact(values):
    return 0.5 * values * (1.0 + lax.erf(values * SQRT_HALF))


def gelu_slope(values):
    return 0.5 * (1.0 + lax.erf(values * SQRT_HALF)) + values * INV_SQRT_TWO_PI * jnp.exp(
        -0.5 * values * values
    )


def normalize(values):
    row_mean = jnp.mean(values, axis=-1, keepdims=True)
    centred = values - row_mean
    inv_std = lax.rsqrt(jnp.mean(centred * centred, axis=-1, keepdims=True) + EPSILON)
    return (centred * inv_std, inv_std)


def norm_back(upstream, normed, inv_std, gain_row):
    scaled = upstream * gain_row
    first_mean = jnp.mean(scaled, axis=-1, keepdims=True)
    second_mean = jnp.mean(scaled * normed, axis=-1, keepdims=True)
    return inv_std * (scaled - first_mean - normed * second_mean)


def contract_rows(left, right):
    return lax.dot_general(
        left, right, (((0,), (0,)), ((), ())), preferred_element_type=jnp.float32
    )


def contract_cols(left, right):
    return lax.dot_general(
        left, right, (((1,), (1,)), ((), ())), preferred_element_type=jnp.float32
    )


def scatter_sum_kernel(parts, count, *refs):
    ins, outs = refs[:count], refs[count : 2 * count]
    first_in, staged, second_in = (refs[(2 + i) * count : (3 + i) * count] for i in range(3))
    send_one, recv_one, send_two, recv_two = refs[5 * count :]
    half = parts // 2
    me = lax.axis_index("dp")
    parity = lax.rem(me, 2)
    place = me // 2
    partner = me + 1 - 2 * parity
    order = list(range(1, half)) + [0]

    barrier = pltpu.get_barrier_semaphore()
    pl.semaphore_signal(
        barrier, inc=1, device_id={"dp": partner}, device_id_type=pl.DeviceIdType.MESH
    )
    for k in range(1, half):
        peer = 2 * lax.rem(place + k, half) + parity
        pl.semaphore_signal(
            barrier, inc=1, device_id={"dp": peer}, device_id_type=pl.DeviceIdType.MESH
        )
    pl.semaphore_wait(barrier, half)

    def each_tile(rows, body):
        def step(i, carry):
            body(pl.ds(pl.multiple_of(i * 16, 16), 16), i)
            return carry

        lax.fori_loop(0, rows // 16, step, 0)

    ones, twos = {}, {}
    for k in order:
        target = lax.rem(place + k, half)
        for i in range(count):
            rows = outs[i].shape[0]
            start = pl.multiple_of((2 * target + 1 - parity) * rows, rows)
            ones[k, i] = pltpu.make_async_remote_copy(
                src_ref=ins[i].at[pl.ds(start, rows)],
                dst_ref=first_in[i].at[k],
                send_sem=send_one.at[i, k],
                recv_sem=recv_one.at[i, k],
                device_id={"dp": partner},
                device_id_type=pl.DeviceIdType.MESH,
            )
            ones[k, i].start()
    for k in order:
        target = lax.rem(place + k, half)
        for i in range(count):
            rows = outs[i].shape[0]
            base = (2 * target + parity) * rows
            ones[k, i].wait_recv()

            def add(tile, step, i=i, k=k, base=base):
                mine = ins[i][pl.ds(pl.multiple_of(base + step * 16, 16), 16), :]
                total = mine.astype(jnp.float32) + first_in[i][k, tile, :].astype(jnp.float32)
                if k:
                    staged[i][k, tile, :] = total.astype(jnp.bfloat16)
                else:
                    outs[i][tile, :] = total

            each_tile(rows, add)
            if k:
                twos[k, i] = pltpu.make_async_remote_copy(
                    src_ref=staged[i].at[k],
                    dst_ref=second_in[i].at[k],
                    send_sem=send_two.at[i, k],
                    recv_sem=recv_two.at[i, k],
                    device_id={"dp": 2 * target + parity},
                    device_id_type=pl.DeviceIdType.MESH,
                )
                twos[k, i].start()
    for i in range(count):
        for k in range(1, half):
            twos[k, i].wait_recv()

        def gather(tile, step, i=i):
            total = outs[i][tile, :]
            for k in range(1, half):
                total = total + second_in[i][k, tile, :].astype(jnp.float32)
            outs[i][tile, :] = total

        each_tile(outs[i].shape[0], gather)
    for copy in list(ones.values()) + list(twos.values()):
        copy.wait_send()


def norms_kernel(
    packed, gain_feat, weight, gain_block, feat_norm, feat_inv, feat_ln, hid_norm, hid_inv, hid_ln
):
    normed, inv = normalize(packed[...].astype(jnp.float32))
    feat_norm[...] = normed
    feat_inv[...] = inv
    scaled = (normed * gain_feat[...]).astype(jnp.bfloat16)
    feat_ln[...] = scaled
    hidden = jnp.dot(scaled, weight[...], preferred_element_type=jnp.float32)
    normed, inv = normalize(hidden)
    hid_norm[...] = normed
    hid_inv[...] = inv
    hid_ln[...] = (normed * gain_block[...]).astype(jnp.bfloat16)


def norms(packed, gain_feat, weight, gain_block):
    rows, channels = packed.shape
    width = weight.shape[1]
    step = min(256, rows)

    def by_row(size):
        return pl.BlockSpec((step, size), lambda i: (i, 0))

    def whole(*shape):
        return pl.BlockSpec(shape, lambda i: (0, 0))

    def made(size, kind):
        return jax.ShapeDtypeStruct((rows, size), kind)

    return pl.pallas_call(
        norms_kernel,
        grid=(rows // step,),
        out_shape=[
            made(channels, jnp.float32), made(1, jnp.float32), made(channels, jnp.bfloat16),
            made(width, jnp.float32), made(1, jnp.float32), made(width, jnp.bfloat16),
        ],
        in_specs=[by_row(channels), whole(1, channels), whole(channels, width), whole(1, width)],
        out_specs=[by_row(size) for size in (channels, 1, channels, width, 1, width)],
        compiler_params=pltpu.CompilerParams(vmem_limit_bytes=VMEM_LIMIT // 2),
        name="norms",
    )(packed, gain_feat[None, :], weight, gain_block[None, :])


def start_copy(src, dst, send_sem, recv_sem, axis, index):
    copy = pltpu.make_async_remote_copy(
        src_ref=src,
        dst_ref=dst,
        send_sem=send_sem,
        recv_sem=recv_sem,
        device_id={axis: index},
        device_id_type=pl.DeviceIdType.MESH,
    )
    copy.start()
    return copy


def greet(peers):
    barrier = pltpu.get_barrier_semaphore()
    for axis, index in peers:
        pl.semaphore_signal(
            barrier, inc=1, device_id={axis: index}, device_id_type=pl.DeviceIdType.MESH
        )
    pl.semaphore_wait(barrier, len(peers))


def block_of(index, size):
    return pl.ds(pl.multiple_of(index * size, size), size)


def product_sum_kernel(parts, count, *refs):
    pairs = [(refs[2 * i], refs[2 * i + 1]) for i in range(count)]
    outs = refs[2 * count : 3 * count]
    made, first_in, staged, second_in = (
        refs[(3 + i) * count : (4 + i) * count] for i in range(4)
    )
    send_one, recv_one, send_two, recv_two = refs[7 * count :]
    half = parts // 2
    d = lax.axis_index("dp")
    parity = lax.rem(d, 2)
    place = d // 2
    partner = d + 1 - 2 * parity
    order = list(range(1, half)) + [0]
    greet(
        [("dp", partner)]
        + [("dp", 2 * lax.rem(place + k, half) + parity) for k in range(1, half)]
    )

    def make(i, index):
        left, right = pairs[i]
        rows = outs[i].shape[0]
        span = block_of(index, rows)
        if rows % 128 == 0:
            piece = left[:, block_of(index, rows)]
            made[i][span, :] = contract_rows(piece, right[...]).astype(jnp.bfloat16)

    def make_all(i):
        left, right = pairs[i]

        def step(t, carry):
            made[i][block_of(t, 128), :] = contract_rows(
                left[:, block_of(t, 128)], right[...]
            ).astype(jnp.bfloat16)
            return carry

        lax.fori_loop(0, left.shape[1] // 128, step, 0)

    def first(i, k):
        rows = outs[i].shape[0]
        target = lax.rem(place + k, half)
        return pltpu.make_async_remote_copy(
            src_ref=made[i].at[block_of(2 * target + 1 - parity, rows)],
            dst_ref=first_in[i].at[k],
            send_sem=send_one.at[i, k],
            recv_sem=recv_one.at[i, k],
            device_id={"dp": partner},
            device_id_type=pl.DeviceIdType.MESH,
        )

    for i in range(count):
        whole = outs[i].shape[0] % 128 != 0
        if whole:
            make_all(i)

        def send(t, carry, i=i, whole=whole):
            k = lax.rem(t + 1, half)
            if not whole:
                make(i, 2 * lax.rem(place + k, half) + 1 - parity)
            first(i, k).start()
            return carry

        lax.fori_loop(0, half, send, 0)

        def keep(t, carry, i=i):
            make(i, 2 * t + parity)
            return carry

        if not whole:
            lax.fori_loop(0, half, keep, 0)

    def each_tile(rows, body):
        def step(t, carry):
            body(block_of(t, 16), t)
            return carry

        lax.fori_loop(0, rows // 16, step, 0)

    twos = {}
    for i in range(count):
        for k in order:
            rows = outs[i].shape[0]
            target = lax.rem(place + k, half)
            base = (2 * target + parity) * rows
            first(i, k).wait_recv()

            def add(tile, step, i=i, k=k, base=base):
                mine = made[i][pl.ds(pl.multiple_of(base + step * 16, 16), 16), :]
                total = mine.astype(jnp.float32) + first_in[i][k, tile, :].astype(jnp.float32)
                if k:
                    staged[i][k, tile, :] = total.astype(jnp.bfloat16)
                else:
                    outs[i][tile, :] = total

            each_tile(rows, add)
            if k:
                twos[i, k] = start_copy(
                    staged[i].at[k],
                    second_in[i].at[k],
                    send_two.at[i, k],
                    recv_two.at[i, k],
                    "dp",
                    2 * target + parity,
                )
    for i in range(count):
        for k in range(1, half):
            twos[i, k].wait_recv()

        def gather(tile, step, i=i):
            total = outs[i][tile, :]
            for k in range(1, half):
                total = total + second_in[i][k, tile, :].astype(jnp.float32)
            outs[i][tile, :] = total

        each_tile(outs[i].shape[0], gather)
    for i in range(count):
        for k in range(half):
            first(i, k).wait_send()
    for copy in twos.values():
        copy.wait_send()


def product_sum(pairs, collective_id):
    parts = lax.axis_size("dp")
    half = parts // 2
    count = len(pairs)
    shapes = [(left.shape[1], right.shape[1]) for left, right in pairs]
    blocks = [(rows // parts, cols) for rows, cols in shapes]
    slots = [pltpu.VMEM((half,) + block, jnp.bfloat16) for block in blocks]
    sent = sum(rows * cols * 2 for rows, cols in shapes)
    return pl.pallas_call(
        functools.partial(product_sum_kernel, parts, count),
        out_shape=[jax.ShapeDtypeStruct(block, jnp.float32) for block in blocks],
        in_specs=[pl.BlockSpec(memory_space=pltpu.VMEM)] * (2 * count),
        out_specs=[pl.BlockSpec(memory_space=pltpu.VMEM)] * count,
        scratch_shapes=[pltpu.VMEM(shape, jnp.bfloat16) for shape in shapes]
        + slots * 3
        + [pltpu.SemaphoreType.DMA((count, half))] * 4,
        compiler_params=pltpu.CompilerParams(
            collective_id=collective_id, has_side_effects=True, vmem_limit_bytes=VMEM_LIMIT
        ),
        cost_estimate=pl.CostEstimate(
            flops=sent * 4000, bytes_accessed=sent * 40, transcendentals=0
        ),
        name="product_sum",
    )(*[value for pair in pairs for value in pair])


def forward_kernel(
    parts, shards, source, packed, arrived, dp_send, dp_recv, near_send, near_recv,
    far_send, far_recv, on_send, on_recv, local
):
    rows, width = source.shape[0] // parts, source.shape[1]
    d = lax.axis_index("dp")
    m = lax.axis_index("mp")
    near = m + 1 - 2 * lax.rem(m, 2)
    fars = shards // 2
    greet(
        [("dp", lax.rem(d + o, parts)) for o in range(1, parts)]
        + [("mp", near)]
        + [("mp", lax.rem(m + 2 * j, shards)) for j in range(1, fars)]
    )
    exchanged, passed, kept = [], [], []
    spans, far_copies = [], []
    for o in range(1, parts):
        target = lax.rem(d + o, parts)
        exchanged.append(
            start_copy(
                source.at[block_of(target, rows)],
                arrived.at[block_of(d, rows)],
                dp_send.at[o],
                dp_recv.at[o],
                "dp",
                target,
            )
        )

    def hand_on(o):
        for j in range(1, fars):
            far_copies[o][j - 1].wait_recv()
            col = block_of(lax.rem(m - 2 * j + shards, shards), width)
            piece = packed.at[spans[o], col]
            passed.append(
                start_copy(piece, piece, on_send.at[o, j], on_recv.at[o, j], "mp", near)
            )

    lag = 2
    nears = []
    for o in range(parts):
        span = block_of(lax.rem(d - o + parts, parts), rows)
        spans.append(span)
        if o:
            exchanged[o - 1].wait_recv()
        block = arrived.at[span] if o else source.at[span]
        mine = packed.at[span, block_of(m, width)]
        far_copies.append(
            [
                start_copy(
                    block, mine, far_send.at[o, j], far_recv.at[o, j], "mp",
                    lax.rem(m + 2 * j, shards),
                )
                for j in range(1, fars)
            ]
        )
        nears.append(start_copy(block, mine, near_send.at[o], near_recv.at[o], "mp", near))
        keep = pltpu.make_async_copy(block, mine, local.at[o])
        keep.start()
        kept.append(keep)
        if o >= lag:
            hand_on(o - lag)
    for o in range(parts - lag, parts):
        hand_on(o)
    for copy in nears + passed:
        copy.wait_recv()
    for copy in kept:
        copy.wait()
    for copy in exchanged + nears + passed + [c for group in far_copies for c in group]:
        copy.wait_send()


def forward_exchange(source, collective_id):
    parts, shards = lax.axis_size("dp"), lax.axis_size("mp")
    rows, width = source.shape
    fars = max(shards // 2, 1)
    return pl.pallas_call(
        functools.partial(forward_kernel, parts, shards),
        out_shape=jax.ShapeDtypeStruct((rows, width * shards), source.dtype),
        in_specs=[pl.BlockSpec(memory_space=pltpu.VMEM)],
        out_specs=pl.BlockSpec(memory_space=pltpu.VMEM),
        scratch_shapes=[pltpu.VMEM((rows, width), source.dtype)]
        + [pltpu.SemaphoreType.DMA((parts,))] * 4
        + [pltpu.SemaphoreType.DMA((parts, fars))] * 4
        + [pltpu.SemaphoreType.DMA((parts,))],
        compiler_params=pltpu.CompilerParams(
            collective_id=collective_id, has_side_effects=True, vmem_limit_bytes=VMEM_LIMIT
        ),
        name="forward_exchange",
    )(source)


def backward_kernel(
    parts, shards, grad, back, middle, mp_send, mp_recv, dp_send, dp_recv, local
):
    share = grad.shape[0]
    rows, width = back.shape[0] // parts, back.shape[1]
    d = lax.axis_index("dp")
    m = lax.axis_index("mp")
    greet(
        [("dp", lax.rem(d + o, parts)) for o in range(1, parts)]
        + [("mp", lax.rem(m + o, shards)) for o in range(1, shards)]
    )
    columns = []
    for o in range(1, shards):
        peer = lax.rem(m + o, shards)
        columns.append(
            start_copy(
                grad.at[:, block_of(peer, width)],
                middle.at[block_of(m, share)],
                mp_send.at[o],
                mp_recv.at[o],
                "mp",
                peer,
            )
        )
    own_column = pltpu.make_async_copy(
        grad.at[:, block_of(m, width)], middle.at[block_of(m, share)], local.at[0]
    )
    own_column.start()

    for copy in columns:
        copy.wait_recv()
    own_column.wait()
    blocks = []
    for o in range(1, parts):
        target = lax.rem(d + o, parts)
        blocks.append(
            start_copy(
                middle.at[block_of(target, rows)],
                back.at[block_of(d, rows)],
                dp_send.at[o],
                dp_recv.at[o],
                "dp",
                target,
            )
        )
    own_block = pltpu.make_async_copy(
        middle.at[block_of(d, rows)], back.at[block_of(d, rows)], local.at[1]
    )
    own_block.start()
    for copy in blocks:
        copy.wait_recv()
    own_block.wait()
    for copy in columns + blocks:
        copy.wait_send()


def backward_exchange(grad, collective_id):
    parts, shards = lax.axis_size("dp"), lax.axis_size("mp")
    share, channels = grad.shape
    back = (share * shards, channels // shards)
    return pl.pallas_call(
        functools.partial(backward_kernel, parts, shards),
        out_shape=jax.ShapeDtypeStruct(back, grad.dtype),
        in_specs=[pl.BlockSpec(memory_space=pltpu.VMEM)],
        out_specs=pl.BlockSpec(memory_space=pltpu.VMEM),
        scratch_shapes=[pltpu.VMEM(back, grad.dtype)]
        + [pltpu.SemaphoreType.DMA((shards,))] * 2
        + [pltpu.SemaphoreType.DMA((parts,))] * 2
        + [pltpu.SemaphoreType.DMA((2,))],
        compiler_params=pltpu.CompilerParams(
            collective_id=collective_id, has_side_effects=True, vmem_limit_bytes=VMEM_LIMIT
        ),
        name="backward_exchange",
    )(grad)


def scatter_sum(terms, collective_id):
    parts = lax.axis_size("dp")
    half = parts // 2
    count = len(terms)
    blocks = [(term.shape[0] // parts, term.shape[1]) for term in terms]
    slots = [pltpu.VMEM((half,) + block, jnp.bfloat16) for block in blocks]
    sent = sum(term.size * 2 for term in terms)
    return pl.pallas_call(
        functools.partial(scatter_sum_kernel, parts, count),
        out_shape=[jax.ShapeDtypeStruct(block, jnp.float32) for block in blocks],
        in_specs=[pl.BlockSpec(memory_space=pltpu.VMEM)] * count,
        out_specs=[pl.BlockSpec(memory_space=pltpu.VMEM)] * count,
        scratch_shapes=slots * 3 + [pltpu.SemaphoreType.DMA((count, half))] * 4,
        compiler_params=pltpu.CompilerParams(
            collective_id=collective_id, has_side_effects=True, vmem_limit_bytes=VMEM_LIMIT
        ),
        cost_estimate=pl.CostEstimate(
            flops=sent * 4000, bytes_accessed=sent * 40, transcendentals=0
        ),
        name="scatter_sum",
    )(*terms)


def on_device(
    conv_in,
    conv_weight,
    feature_gain,
    proj_weight,
    block_gain,
    w_in,
    w_out,
    cotangent,
    send_index,
    slot_valid,
):
    frames = conv_in.shape[0]
    shards = lax.axis_size("mp")
    member = lax.axis_index("mp")
    pre_act = jnp.dot(conv_in, conv_weight, preferred_element_type=jnp.float32)
    features = gelu_exact(pre_act).astype(jnp.bfloat16)
    choose = (send_index[:, None] == jnp.arange(frames, dtype=send_index.dtype)).astype(jnp.bfloat16)
    outgoing = jnp.dot(choose, features, preferred_element_type=jnp.float32).astype(jnp.bfloat16)
    packed = forward_exchange(outgoing, 3)
    feat_norm, feat_inv, feat_ln, hid_norm, hid_inv, hid_ln = norms(
        packed, feature_gain, proj_weight, block_gain
    )
    upward = jnp.dot(hid_ln, w_in, preferred_element_type=jnp.float32)
    valid = slot_valid.astype(jnp.float32)[:, None]
    active = (valid * gelu_exact(upward)).astype(jnp.bfloat16)
    grad_active = valid * jnp.dot(cotangent, w_out, preferred_element_type=jnp.float32)
    grad_upward = (grad_active * gelu_slope(upward)).astype(jnp.bfloat16)
    partial_value = contract_cols(grad_upward, w_in)
    share_rows = frames // shards
    first_row = member * share_rows
    share_normed = lax.psum_scatter(
        partial_value.astype(jnp.bfloat16), "mp", scatter_dimension=0, tiled=True
    ).astype(jnp.float32)
    out_grad, in_grad = product_sum([(cotangent, active), (hid_ln, grad_upward)], 1)
    share_normed, in_grad, out_grad = lax.optimization_barrier((share_normed, in_grad, out_grad))
    share_cot = lax.dynamic_slice_in_dim(valid, first_row, share_rows, 0) * (
        lax.dynamic_slice_in_dim(cotangent, first_row, share_rows, 0).astype(jnp.float32)
    )
    share_norm = lax.dynamic_slice_in_dim(hid_norm, first_row, share_rows, 0)
    share_inv = lax.dynamic_slice_in_dim(hid_inv, first_row, share_rows, 0)
    share_grad = (share_cot + norm_back(share_normed, share_norm, share_inv, block_gain)).astype(
        jnp.bfloat16
    )
    share_feat = lax.dynamic_slice_in_dim(feat_ln, first_row, share_rows, 0)
    share_feat_norm = lax.dynamic_slice_in_dim(feat_norm, first_row, share_rows, 0)
    share_feat_inv = lax.dynamic_slice_in_dim(feat_inv, first_row, share_rows, 0)
    grad_feat_ln = contract_cols(share_grad, proj_weight)
    grad_packed = norm_back(grad_feat_ln, share_feat_norm, share_feat_inv, feature_gain).astype(
        jnp.bfloat16
    )
    proj_term = contract_rows(share_feat, share_grad)
    proj_part = lax.psum_scatter(
        proj_term.astype(jnp.bfloat16), "mp", scatter_dimension=1, tiled=True
    )
    returned = backward_exchange(grad_packed, 4)
    grad_features = contract_rows(choose, returned)
    grad_pre = (grad_features * gelu_slope(pre_act)).astype(jnp.bfloat16)
    conv_term = contract_rows(conv_in, grad_pre)
    conv_grad, proj_grad = scatter_sum([conv_term.astype(jnp.bfloat16), proj_part], 2)
    grads = (conv_grad, proj_grad, in_grad, out_grad)
    result = (grads[0], grads[1], grads[2], grads[3])
    return result


def solution(mesh):
    placed = (
        P("dp", None),
        P(None, "mp"),
        P(),
        P(),
        P(),
        P(None, "mp"),
        P(None, "mp"),
        P("dp", None),
        P("dp"),
        P("dp"),
    )
    return jax.shard_map(
        on_device,
        mesh=mesh,
        in_specs=placed,
        out_specs=(P("dp", "mp"), P("dp", "mp"), P("dp", "mp"), P("dp", "mp")),
        check_vma=False,
    )
```
